32 devices in a mesh: row: 2 (over x), col: 4 (over y, core), freq: 4 (over z).
Axes of the slice: x: 2, y: 2, z: 4, core: 2. Of those that a mesh axis runs over, the one named last changes fastest.
Arguments:
- covariance: bfloat16 [16, 2, 4096, 4096], P('freq', None, 'row', 'col'), may hold values from -30 to 30, as said below
- replica_table: bfloat16 [16, 2, 4096, 512], P('freq', None, 'col'), may hold values from -18 to 18
- slab_index: int32 [384], replicated, may hold values from 0 to 511
Outputs:
- power: float32 [16, 384], P('freq', ('row', 'col'))
- surface: float32 [384], P(('row', 'col'))
The draws below stay inside these ranges and needn't reach their ends.
Inputs may be any that keep to these rules, and one draw needn't show every extreme that they name: For each frequency, covariance is Hermitian: its real part is symmetric and its imaginary part antisymmetric, and the whole is positive definite.
All inputs are finite; a program needn't handle non-finite values.
Results may differ from the reference program's by a relative error of at most 0.0003.
Values may be sent and summed in bfloat16 or wider, within the bound.
No kernel may reach another device: no remote copies, remote signals or barrier semaphores. Data moves between devices by JAX's collectives and lax.ppermute only.
A program may use at most 192 MiB of HBM per device.

```python
import math
import jax
import jax.numpy as jnp
from jax import lax

CH = 4096
FREQ = 16
SLAB = 384
TABLE = 512


noise_floor = 0.6


coupling = 0.1


sources = 8


def draw_covariance(key, part):
    spread = coupling / math.sqrt(CH)

    def one_frequency(index):
        subkey = jax.random.fold_in(key, index)
        key_sym = jax.random.fold_in(subkey, 0)
        key_anti = jax.random.fold_in(subkey, 1)
        key_gain = jax.random.fold_in(subkey, 2)
        key_phase = jax.random.fold_in(subkey, 3)
        key_power = jax.random.fold_in(subkey, 5)
        symmetric = jax.random.normal(key_sym, (CH, CH), jnp.float32)
        antisym = jax.random.normal(key_anti, (CH, CH), jnp.float32)
        gains = jnp.exp(jax.random.uniform(key_gain, (CH,), jnp.float32, 0.0, math.log(100.0))) / 10.0
        strength = jnp.exp(jax.random.uniform(key_power, (sources,), jnp.float32, math.log(0.03), math.log(0.25)))
        phase = jax.random.uniform(key_phase, (CH, sources), jnp.float32, -math.pi, math.pi)
        root_power = jnp.sqrt(strength)[None, :]
        cosine = jnp.cos(phase) * root_power
        sine = jnp.sin(phase) * root_power
        source_real = jnp.dot(cosine, cosine.T) + jnp.dot(sine, sine.T)
        source_imag = jnp.dot(sine, cosine.T) - jnp.dot(cosine, sine.T)
        scales = jnp.sqrt(gains)
        outer = scales[:, None] * scales[None, :]
        real_part = (noise_floor * jnp.eye(CH, dtype=jnp.float32) + spread * (symmetric + symmetric.T) + source_real) * outer
        imag_part = (spread * (antisym - antisym.T) + source_imag) * outer
        return jnp.stack([real_part, imag_part]).astype(jnp.bfloat16)
    return lax.map(one_frequency, jnp.arange(FREQ))


def draw_replica_table(key, part):
    key_amp, key_phase = jax.random.split(jax.random.fold_in(key, 7))
    channel = jnp.arange(CH).astype(jnp.float32) / CH
    rising = 3.0 ** channel
    amplitude = jnp.exp(jax.random.uniform(key_amp, (FREQ, CH, TABLE), jnp.float32, math.log(0.5), math.log(2.0)))
    magnitude = amplitude * rising[None, :, None]
    phase = jax.random.uniform(key_phase, (FREQ, CH, TABLE), jnp.float32, -math.pi, math.pi)
    return jnp.stack([magnitude * jnp.cos(phase), magnitude * jnp.sin(phase)], axis=1).astype(jnp.bfloat16)


def touch_ends(values, own_key, low, largest):
    extent = values.shape
    place = [jax.random.randint(jax.random.fold_in(own_key, axis), (), 0, extent[axis]) for axis in range(len(extent))]
    values = values.at[tuple(place)].set(low)
    longest = extent.index(max(extent))
    place[longest] = (place[longest] + 1) % extent[longest]
    return values.at[tuple(place)].set(largest)


def setup_inputs(seed: int = 0) -> dict:
    arg_keys = jax.random.split(jax.random.key(seed), 4)
    covariance = draw_covariance(jax.random.fold_in(arg_keys[3], 71), 0)
    replica_table = draw_replica_table(jax.random.fold_in(arg_keys[3], 71), 0)
    slab_index = touch_ends(jax.random.randint(arg_keys[2], (SLAB,), 0, TABLE), jax.random.fold_in(arg_keys[2], 1), 0, TABLE - 1).astype(jnp.int32)
    return dict(covariance=covariance, replica_table=replica_table, slab_index=slab_index)


def reference(covariance, replica_table, slab_index):
    def one_frequency(index):
        matrix = covariance[index]
        table = replica_table[index]
        replica = jnp.take(table, slab_index, axis=2)
        part_a = replica[0]
        part_b = replica[1]
        real_a = jnp.dot(matrix[0], part_a, preferred_element_type=jnp.float32)
        real_b = jnp.dot(matrix[0], part_b, preferred_element_type=jnp.float32)
        imag_a = jnp.dot(matrix[1], part_a, preferred_element_type=jnp.float32)
        imag_b = jnp.dot(matrix[1], part_b, preferred_element_type=jnp.float32)
        image_real = real_a - imag_b
        image_imag = real_b + imag_a
        wide_a = part_a.astype(jnp.float32)
        wide_b = part_b.astype(jnp.float32)
        quad = jnp.sum(wide_a * image_real + wide_b * image_imag, axis=0)
        weight = jnp.sum(wide_a * wide_a + wide_b * wide_b, axis=0)
        return quad / weight

    power = lax.map(one_frequency, jnp.arange(FREQ))
    surface = jnp.sum(power, axis=0) / FREQ
    return power, surface
```

```python
import functools

import jax
import jax.numpy as jnp
from jax import lax
from jax.experimental import pallas as pl
from jax.experimental.pallas import tpu as pltpu
from jax.sharding import PartitionSpec as P


RELAYED = 2


class Place:
    def __init__(self, freqs):
        row, col = lax.axis_index("row"), lax.axis_index("col")
        chip, core = col // 2, col % 2
        half = freqs // 2
        self.diag = row == chip
        self.on = (row == chip).astype(jnp.int32)
        self.core = core
        self.first = jnp.where(row == chip, core, (row > chip).astype(jnp.int32)) * half
        self.other = half - self.first
        self.row, self.chip, self.half = row, chip, half

    def sends(self, d, rows):
        to = (self.row + d) % rows
        direct = (self.row > to).astype(jnp.int32) * self.half
        relay = (self.chip > self.row).astype(jnp.int32) * self.half + self.half // 2
        return jnp.where(self.diag, direct, relay)


def dot(x, y):
    return jnp.dot(x, y, preferred_element_type=jnp.float32)


def row_sum(x):
    return jnp.sum(x, axis=0, keepdims=True)


def onehot_of(index_ref, grid_points):
    slab = index_ref.shape[0]
    points = lax.broadcasted_iota(jnp.int32, (grid_points, slab), 0)
    hit = points == index_ref[...].reshape(1, slab)
    return jnp.where(hit, 1.0, 0.0).astype(jnp.bfloat16)


def pick_kernel(sizes, index_ref, main_ref, extra_ref, *out_refs):
    slab = index_ref.shape[0]
    onehot = onehot_of(index_ref, main_ref.shape[3])
    start = 0
    for size, out_ref in zip(sizes, out_refs, strict=True):
        twice = out_ref.shape[0] > size
        for part in range(2):
            columns = slice(part * slab, (part + 1) * slab)
            piece = dot(main_ref[0, part, start : start + size], onehot)
            out_ref[:size, columns] = piece.astype(jnp.bfloat16)
            if twice:
                piece = dot(extra_ref[0, part], onehot)
                out_ref[size:, columns] = piece.astype(jnp.bfloat16)
        start += size


def pick(index, table, d, rows, start, sizes, double_last):
    freqs, _, block, grid_points = table.shape
    slab = index.shape[0]
    height = sum(sizes)
    shapes = [(n, 2 * slab) for n in sizes]
    if double_last:
        shapes[-1] = (2 * sizes[-1], 2 * slab)
    extra = sizes[-1] if double_last else 16
    quarter = freqs // 4

    def main_at(i):
        return (Place(freqs).sends(d, rows), 0, start, 0)

    def extra_at(i):
        place = Place(freqs)
        return (jnp.where(place.diag, place.sends(d, rows) + quarter, 0), 0, block - extra, 0)

    def rows_of(height, at):
        element = pl.Element
        return pl.BlockSpec((element(1), element(2), element(height), element(grid_points)), at)

    return pl.pallas_call(
        functools.partial(pick_kernel, sizes),
        grid=(1,),
        in_specs=[pl.BlockSpec((slab,), lambda i: (0,)), rows_of(height, main_at), rows_of(extra, extra_at)],
        out_specs=[pl.BlockSpec(s, lambda i: (0, 0)) for s in shapes],
        out_shape=[jax.ShapeDtypeStruct(s, jnp.bfloat16) for s in shapes],
    )(index, table, table)


def gather_kernel(index_ref, table_ref, w_ref, norm_ref, onehot_ref):
    f = pl.program_id(0)
    slab = index_ref.shape[0]

    @pl.when(f == 0)
    def _():
        onehot_ref[...] = onehot_of(index_ref, table_ref.shape[3])

    total = jnp.zeros((1, slab), jnp.float32)
    for part in range(2):
        piece = dot(table_ref[0, part], onehot_ref[...])
        w_ref[0, :, part * slab : (part + 1) * slab] = piece.astype(jnp.bfloat16)
        total += row_sum(piece * piece)
    norm_ref[pl.ds(f, 1), :] = total


def gather(index, table):
    freqs, _, block, grid_points = table.shape
    slab = index.shape[0]
    return pl.pallas_call(
        gather_kernel,
        grid=(freqs,),
        in_specs=[
            pl.BlockSpec((slab,), lambda f: (0,)),
            pl.BlockSpec((1, 2, block, grid_points), lambda f: (f, 0, 0, 0)),
        ],
        out_specs=[
            pl.BlockSpec((1, block, 2 * slab), lambda f: (f, 0, 0)),
            pl.BlockSpec((freqs, slab), lambda f: (0, 0)),
        ],
        out_shape=[
            jax.ShapeDtypeStruct((freqs, block, 2 * slab), jnp.bfloat16),
            jax.ShapeDtypeStruct((freqs, slab), jnp.float32),
        ],
        scratch_shapes=[pltpu.VMEM((grid_points, slab), jnp.bfloat16)],
        name="gather",
    )(index, table)


def turned(w_ref, w2_ref, start=0):
    slab = w2_ref.shape[1] // 2
    w2_ref[start:, :slab] = -w_ref[0, start:, slab:]
    w2_ref[start:, slab:] = w_ref[0, start:, :slab]


def image_of(cov_ref, w_ref, w2_ref):
    turned(w_ref, w2_ref)
    return dot(cov_ref[0, 0], w_ref[0]) + dot(cov_ref[0, 1], w2_ref[...])


def send_kernel(cov_ref, w_ref, image_ref, w2_ref):
    image_ref[0] = image_of(cov_ref, w_ref, w2_ref)


def send_images(covariance, w):
    freqs, block, wide = w.shape
    half = freqs // 2

    def cov_at(i):
        place = Place(freqs)
        return (place.first + i, 0, 1 - place.core, 0)

    return pl.pallas_call(
        send_kernel,
        grid=(half,),
        in_specs=[
            pl.BlockSpec((1, 2, block, block), cov_at),
            pl.BlockSpec((1, block, wide), lambda i: (Place(freqs).first + i, 0, 0)),
        ],
        out_specs=pl.BlockSpec((1, block, wide), lambda i: (i, 0, 0)),
        scratch_shapes=[pltpu.VMEM((block, wide), jnp.bfloat16)],
        out_shape=jax.ShapeDtypeStruct((half, block, wide), jnp.float32),
        name="send_images",
    )(covariance, w)


def own_form(cov_ref, w_ref, w2_ref):
    block, wide = w2_ref.shape
    slab = wide // 2
    tile = block // 2
    turned(w_ref, w2_ref, tile)
    total = jnp.zeros((1, wide), jnp.float32)
    for t in range(2):
        rows = slice(t * tile, (t + 1) * tile)
        left = w_ref[0, rows].astype(jnp.float32)
        image = dot(cov_ref[0, 0, rows, rows], w_ref[0, rows])
        cross = dot(cov_ref[0, 1, rows, rows], w_ref[0, rows, :slab])
        if t == 0:
            rest = slice(tile, block)
            upper = dot(cov_ref[0, 0, rows, rest], w_ref[0, rest])
            upper += dot(cov_ref[0, 1, rows, rest], w2_ref[rest])
            image += 2.0 * upper
        total += row_sum(left * image)
        twice = 2.0 * row_sum(left[:, slab:] * cross)
        total += jnp.concatenate([twice, jnp.zeros_like(twice)], axis=1)
    return total


def keep_kernel(cov_ref, w_ref, image_ref, quad_ref, w2_ref):
    i = pl.program_id(0)
    freqs = quad_ref.shape[0]
    place = Place(freqs)

    @pl.when(i == 0)
    def _():
        quad_ref[...] = jnp.zeros_like(quad_ref)

    @pl.when(place.diag)
    def _():
        quad_ref[pl.ds(i, 1), :] = own_form(cov_ref, w_ref, w2_ref)

    @pl.when(jnp.logical_not(place.diag) & (i < freqs // 2))
    def _():
        image_ref[0] = image_of(cov_ref, w_ref, w2_ref)


def keep_images(covariance, w):
    freqs, block, wide = w.shape
    half = freqs // 2

    def freq_at(i):
        place = Place(freqs)
        return jnp.where(place.diag, i, place.first + jnp.minimum(i, half - 1))

    return pl.pallas_call(
        keep_kernel,
        grid=(freqs,),
        in_specs=[
            pl.BlockSpec((1, 2, block, block), lambda i: (freq_at(i), 0, Place(freqs).core, 0)),
            pl.BlockSpec((1, block, wide), lambda i: (freq_at(i), 0, 0)),
        ],
        out_specs=[
            pl.BlockSpec(
                (1, block, wide), lambda i: (jnp.minimum(i, half - 1) * (1 - Place(freqs).on), 0, 0)
            ),
            pl.BlockSpec((freqs, wide), lambda i: (0, 0)),
        ],
        scratch_shapes=[pltpu.VMEM((block, wide), jnp.bfloat16)],
        out_shape=[
            jax.ShapeDtypeStruct((half, block, wide), jnp.float32),
            jax.ShapeDtypeStruct((freqs, wide), jnp.float32),
        ],
        name="keep_images",
    )(covariance, w)


def fetch_all(pieces, keep_ref, received_ref, buffers, sems):
    copies = []
    for k, (_, _, rows, item, row) in enumerate(pieces):
        for s, side in enumerate((keep_ref, received_ref)):
            copy = pltpu.make_async_copy(side.at[item, pl.ds(row, rows)], buffers[2 * k + s], sems.at[2 * k + s])
            copy.start()
            copies.append(copy)
    return copies


def add_far(pieces, lefts, copies, buffers, quad_ref, first):
    for k, (source, at, rows, item, _) in enumerate(pieces):
        for s in range(2):
            copies[2 * k + s].wait()
        left = lefts[source][at : at + rows].astype(jnp.float32)
        value = 2.0 * row_sum(left * (buffers[2 * k][...] + buffers[2 * k + 1][...]))
        quad_ref[pl.ds(first + item, 1), :] += value


def early_kernel(pieces, n_left, quad_in_ref, w_ref, keep_ref, received_ref, *refs):
    lefts, (out_ref, w_buffer, image_buffer, own_sems, sems), buffers = (
        refs[:n_left],
        refs[n_left : n_left + 5],
        refs[n_left + 5 :],
    )
    freqs, half = w_ref.shape[0], received_ref.shape[0]
    place = Place(freqs)
    out_ref[...] = quad_in_ref[...]

    @pl.when(place.diag)
    def _():
        copies = []
        for i in range(half):
            copies.append(pltpu.make_async_copy(w_ref.at[place.other + i], w_buffer.at[i], own_sems.at[2 * i]))
            copies.append(pltpu.make_async_copy(received_ref.at[i], image_buffer.at[i], own_sems.at[2 * i + 1]))
        for copy in copies:
            copy.start()
        for i in range(half):
            copies[2 * i].wait()
            copies[2 * i + 1].wait()
            value = 2.0 * row_sum(w_buffer[i].astype(jnp.float32) * image_buffer[i])
            out_ref[pl.ds(place.other + i, 1), :] += value

    @pl.when(jnp.logical_not(place.diag))
    def _():
        copies = fetch_all(pieces, keep_ref, received_ref, buffers, sems)
        add_far(pieces, lefts, copies, buffers, out_ref, place.first)


HBM = pl.BlockSpec(memory_space=pltpu.HBM)
VMEM = pl.BlockSpec(memory_space=pltpu.VMEM)


def piece_buffers(pieces, wide):
    return [pltpu.VMEM((p[2], wide), jnp.float32) for p in pieces for _ in range(2)]


def early_dots(quad, w, keep, received, lefts, pieces):
    _, block, wide = w.shape
    half = received.shape[0]
    return pl.pallas_call(
        functools.partial(early_kernel, pieces, len(lefts)),
        in_specs=[VMEM, HBM, HBM, HBM] + [VMEM] * len(lefts),
        out_specs=VMEM,
        scratch_shapes=[
            pltpu.VMEM((half, block, wide), jnp.bfloat16),
            pltpu.VMEM((half, block, wide), jnp.float32),
            pltpu.SemaphoreType.DMA((2 * half,)),
            pltpu.SemaphoreType.DMA((2 * len(pieces),)),
            *piece_buffers(pieces, wide),
        ],
        out_shape=jax.ShapeDtypeStruct(quad.shape, jnp.float32),
        name="early_dots",
    )(quad, w, keep, received, *lefts)


def late_kernel(pieces, n_left, planes, quad_in_ref, norm_ref, keep_ref, received_ref, *refs):
    lefts, (out_ref, quad_ref, sems), buffers = refs[:n_left], refs[n_left : n_left + 3], refs[n_left + 3 :]
    freqs, slab = norm_ref.shape
    place = Place(freqs)
    quad_ref[...] = quad_in_ref[...]

    @pl.when(jnp.logical_not(place.diag))
    def _():
        copies = fetch_all(pieces, keep_ref, received_ref, buffers, sems)
        add_far(pieces, lefts, copies, buffers, quad_ref, place.first)

    both = jnp.concatenate([quad_ref[:, :slab] + quad_ref[:, slab:], norm_ref[...]], axis=0)
    own = out_ref.shape[2]
    for owner in range(out_ref.shape[0] // planes):
        parcel = both[:, owner * own : (owner + 1) * own]
        for z in range(planes):
            out_ref[owner * planes + z] = parcel


def late_dots(quad, norm, keep, received, lefts, pieces, owners, planes):
    freqs, slab = norm.shape
    wide = quad.shape[1]
    return pl.pallas_call(
        functools.partial(late_kernel, pieces, len(lefts), planes),
        in_specs=[VMEM, VMEM, HBM, HBM] + [VMEM] * len(lefts),
        out_specs=VMEM,
        scratch_shapes=[
            pltpu.VMEM((freqs, wide), jnp.float32),
            pltpu.SemaphoreType.DMA((2 * len(pieces),)),
            *piece_buffers(pieces, wide),
        ],
        out_shape=jax.ShapeDtypeStruct((owners * planes, 2 * freqs, slab // owners), jnp.float32),
        name="late_dots",
    )(quad, norm, keep, received, *lefts)


def finish_kernel(planes, copies, arrived_ref, power_ref, surface_ref):
    freqs = power_ref.shape[0]
    mine = lax.axis_index("freq")
    surface = jnp.zeros_like(surface_ref)
    for z in range(planes):
        total = arrived_ref[z]
        for source in range(1, arrived_ref.shape[0] // planes):
            total += arrived_ref[source * planes + z]
        power = total[:freqs] / (total[freqs:] * (1.0 / copies))
        surface += row_sum(power)

        @pl.when(mine == z)
        def _():
            power_ref[...] = power

    surface_ref[...] = surface / (freqs * planes)


def finish(arrived, planes, copies):
    _, twice, own = arrived.shape
    return pl.pallas_call(
        functools.partial(finish_kernel, planes, copies),
        in_specs=[VMEM],
        out_specs=[VMEM, VMEM],
        out_shape=[
            jax.ShapeDtypeStruct((twice // 2, own), jnp.float32),
            jax.ShapeDtypeStruct((1, own), jnp.float32),
        ],
        name="finish",
    )(arrived)


def local(mesh, covariance, replica_table, slab_index):
    rows, cols, planes = (mesh.shape[a] for a in ("row", "col", "freq"))
    freqs, _, row_block, block = covariance.shape
    chips = cols // 2
    if row_block != 2 * block or chips != rows or freqs != 4:
        raise ValueError("unsupported mesh")
    axes = ("row", "col")

    def device(r, q, j):
        return r * cols + 2 * q + j

    def move(x, pairs):
        return lax.ppermute(x, axes, pairs)

    def total(xs):
        return functools.reduce(jnp.add, xs)

    everyone = [(r, q, j) for r in range(rows) for q in range(chips) for j in range(2)]
    core_swap = [(device(r, q, j), device(r, q, 1 - j)) for r, q, j in everyone]

    n = RELAYED
    chunk = block * 2 // 5 // 16 * 16
    tail = block - n * chunk
    shifts = range(1, rows)
    pairs = {}
    for d in shifts:
        out, back, relay = [], [], []
        for r in range(rows):
            for j in range(2):
                other = (r + d) % rows
                out.append((device(r, r, j), device(r, other, j)))
                back.append((device(r, other, j), device(r, r, j)))
                relay.append((device(r, r, j), device(other, r, j)))
        pairs[d] = out, out + back, relay

    chunks, hops = {}, {}
    for d in shifts:
        chunks[d] = pick(slab_index, replica_table, d, rows, 0, [chunk], False)
        hops[d] = [move(chunks[d][0], pairs[d][1])]
    for d in shifts:
        sizes = [chunk] * (n - 1) + [tail]
        chunks[d] += pick(slab_index, replica_table, d, rows, chunk, sizes, True)
        for k in range(1, n + 1):
            hops[d].append(move(chunks[d][k], pairs[d][1 if k < n else 0]))

    w, norm = gather(slab_index, replica_table)
    sent = send_images(covariance, w)
    received = move(sent, core_swap)
    relayed = [total([move(hops[d][k], pairs[d][2]) for d in shifts]) for k in range(n)]
    direct = [total([hops[d][k] for d in shifts]) for k in range(n + 1)]
    keep, quad = keep_images(covariance, w)
    early = [(k, 0, chunk, 0, k * chunk) for k in range(n)]
    early += [(n + k, 0, chunk, 1, k * chunk) for k in range(n - 1)]
    late = [(0, 0, tail, 0, n * chunk), (0, tail, tail, 1, n * chunk), (1, 0, chunk, 1, (n - 1) * chunk)]
    quad = early_dots(quad, w, keep, received, direct[:n] + relayed[: n - 1], early)
    parcels = late_dots(
        quad, norm, keep, received, [direct[n], relayed[-1]], late, rows * cols, planes
    )
    arrived = lax.all_to_all(parcels, ("row", "col", "freq"), 0, 0)
    power, surface = finish(arrived, planes, rows)
    return power, surface[0]


def solution(mesh):
    in_specs = (P("freq", None, "row", "col"), P("freq", None, "col", None), P())
    out_specs = (P("freq", ("row", "col")), P(("row", "col")))

    def body(covariance, replica_table, slab_index):
        return local(mesh, covariance, replica_table, slab_index)

    return jax.shard_map(body, mesh=mesh, in_specs=in_specs, out_specs=out_specs, check_vma=False)
```

```python
import functools

import jax
import jax.numpy as jnp
from jax import lax
from jax.experimental import pallas as pl
from jax.experimental.pallas import tpu as pltpu
from jax.sharding import PartitionSpec as P


CHUNKS = (4, 5, 4)
RELAYED = len(CHUNKS)


PARAMS = pltpu.CompilerParams(vmem_limit_bytes=30 << 20)


HBM = pl.BlockSpec(memory_space=pltpu.HBM)
VMEM = pl.BlockSpec(memory_space=pltpu.VMEM)


def apart(x):
    return pltpu.with_memory_space_constraint(x, pltpu.HBM)


def resident(x):
    return pltpu.with_memory_space_constraint(x, pltpu.VMEM)


class Place:
    def __init__(self, freqs):
        row, col = lax.axis_index("row"), lax.axis_index("col")
        chip, core = col // 2, col % 2
        half = freqs // 2
        self.diag = row == chip
        self.on = (row == chip).astype(jnp.int32)
        self.core = core
        self.first = jnp.where(row == chip, core, (row > chip).astype(jnp.int32)) * half
        self.other = half - self.first
        self.row, self.chip, self.half = row, chip, half

    def sends(self, d, rows):
        to = (self.row + d) % rows
        direct = (self.row > to).astype(jnp.int32) * self.half
        relay = (self.chip > self.row).astype(jnp.int32) * self.half + self.half // 2
        return jnp.where(self.diag, direct, relay)


def dot(x, y):
    return jnp.dot(x, y, preferred_element_type=jnp.float32)


def row_sum(x):
    return jnp.sum(x, axis=0, keepdims=True)


def folded(rows, wide, product):
    def step(k, total):
        part = product(pl.multiple_of(k * 16, 16), 16)
        return total + (part[:8] + part[8:])

    return row_sum(lax.fori_loop(0, rows // 16, step, jnp.zeros((8, wide), jnp.float32), unroll=4))


def onehot_of(index_ref, grid_points):
    slab = index_ref.shape[0]
    points = lax.broadcasted_iota(jnp.int32, (grid_points, slab), 0)
    hit = points == index_ref[...].reshape(1, slab)
    return jnp.where(hit, 1.0, 0.0).astype(jnp.bfloat16)


def pick_kernel(sizes, index_ref, main_ref, *refs):
    slab = index_ref.shape[0]
    extra_ref, out_refs = (refs[0], refs[1:]) if len(refs) > len(sizes) else (None, refs)
    onehot = onehot_of(index_ref, main_ref.shape[3])
    start = 0
    for size, out_ref in zip(sizes, out_refs, strict=True):
        for part in range(2):
            columns = slice(part * slab, (part + 1) * slab)
            piece = dot(main_ref[0, part, start : start + size], onehot)
            out_ref[:size, columns] = piece.astype(jnp.bfloat16)
            if out_ref.shape[0] > size:
                piece = dot(extra_ref[0, part], onehot)
                out_ref[size:, columns] = piece.astype(jnp.bfloat16)
        start += size


def pick(index, table, d, rows, start, sizes, double_last):
    freqs, _, _, grid_points = table.shape
    slab = index.shape[0]
    shapes = [(n, 2 * slab) for n in sizes]
    height = sum(sizes)
    extra = sizes[-1]
    quarter = freqs // 4

    def main_at(i):
        return (Place(freqs).sends(d, rows), 0, start, 0)

    def extra_at(i):
        place = Place(freqs)
        return (jnp.where(place.diag, place.sends(d, rows) + quarter, 0), 0, start + height - extra, 0)

    def rows_of(height, at):
        element = pl.Element
        return pl.BlockSpec((element(1), element(2), element(height), element(grid_points)), at)

    specs = [pl.BlockSpec((slab,), lambda i: (0,)), rows_of(height, main_at)]
    args = [index, table]
    if double_last:
        shapes[-1] = (2 * extra, 2 * slab)
        specs.append(rows_of(extra, extra_at))
        args.append(table)
    return pl.pallas_call(
        functools.partial(pick_kernel, sizes),
        grid=(1,),
        in_specs=specs,
        out_specs=[pl.BlockSpec(s, lambda i: (0, 0)) for s in shapes],
        out_shape=[jax.ShapeDtypeStruct(s, jnp.bfloat16) for s in shapes],
        compiler_params=PARAMS,
    )(*args)


class Stream:
    def __init__(self, copies):
        self.copies = [pltpu.make_async_copy(*copy) for copy in copies]
        self.copies[0].start()
        self.taken = 0

    def take(self):
        self.copies[self.taken].wait()
        self.taken += 1
        if self.taken < len(self.copies):
            self.copies[self.taken].start()


def gather_kernel(index_ref, table_ref, w_ref, norm_ref, onehot_ref, buffer, sems):
    slab = index_ref.shape[0]
    freqs = norm_ref.shape[0]
    place = Place(freqs)

    def work(steps, at, with_norm):
        stream = Stream([(table_ref.at[at(i)], buffer.at[i], sems.at[i]) for i in range(steps)])
        onehot_ref[...] = onehot_of(index_ref, table_ref.shape[3])
        for i in range(steps):
            stream.take()
            total = jnp.zeros((1, slab), jnp.float32)
            for part in range(2):
                piece = dot(buffer[i, part], onehot_ref[...])
                w_ref[at(i), :, part * slab : (part + 1) * slab] = piece.astype(jnp.bfloat16)
                if with_norm:
                    total += row_sum(piece * piece)
            if with_norm:
                norm_ref[i : i + 1, :] = total

    @pl.when(place.diag)
    def _():
        work(freqs, lambda i: i, True)

    @pl.when(jnp.logical_not(place.diag))
    def _():
        norm_ref[...] = jnp.zeros_like(norm_ref)
        work(freqs // 2, lambda i: place.first + i, False)


def gather(index, table):
    freqs, _, block, grid_points = table.shape
    slab = index.shape[0]
    return pl.pallas_call(
        gather_kernel,
        in_specs=[VMEM, HBM],
        out_specs=[VMEM, VMEM],
        out_shape=[
            jax.ShapeDtypeStruct((freqs, block, 2 * slab), jnp.bfloat16),
            jax.ShapeDtypeStruct((freqs, slab), jnp.float32),
        ],
        scratch_shapes=[
            pltpu.VMEM((grid_points, slab), jnp.bfloat16),
            pltpu.VMEM((freqs, 2, block, grid_points), jnp.bfloat16),
            pltpu.SemaphoreType.DMA((freqs,)),
        ],
        name="gather",
        compiler_params=PARAMS,
    )(resident(index), table)


def turned(w, w2_ref, start=0):
    slab = w2_ref.shape[1] // 2
    w2_ref[start:, :slab] = -w[start:, slab:]
    w2_ref[start:, slab:] = w[start:, :slab]


def block_stream(items, first, side, cov_ref, buffer, sems, triangle):
    block = buffer.shape[2]
    tile = block // 2
    copies = []
    for i in items:
        for t in range(2):
            rows = pl.ds(pl.multiple_of(side * block + t * tile, tile), tile)
            columns = pl.ds(tile, tile) if triangle and t else pl.ds(0, block)
            target = buffer.at[i, :, pl.ds(t * tile, tile), columns]
            copies.append((cov_ref.at[first + i, :, rows, columns], target, sems.at[2 * i + t]))
    return Stream(copies)


def images_of(items, first, side, cov_ref, w_ref, image_ref, buffer, w2_ref, sems):
    stream = block_stream(items, first, side, cov_ref, buffer, sems, False)
    tile = buffer.shape[2] // 2
    for place, i in enumerate(items):
        w = w_ref.at[first + i]
        turned(w, w2_ref)
        for t in range(2):
            stream.take()
            rows = slice(t * tile, (t + 1) * tile)
            image_ref[place, rows] = dot(buffer[i, 0, rows], w[...]) + dot(buffer[i, 1, rows], w2_ref[...])


def send_kernel(cov_ref, w_ref, image_ref, buffer, w2_ref, sems):
    place = Place(w_ref.shape[0])
    images_of(range(image_ref.shape[0]), place.first, 1 - place.core, cov_ref, w_ref, image_ref, buffer, w2_ref, sems)


def block_scratch(half, block, wide):
    return [
        pltpu.VMEM((half, 2, block, block), jnp.bfloat16),
        pltpu.VMEM((block, wide), jnp.bfloat16),
        pltpu.SemaphoreType.DMA((2 * half,)),
    ]


def send_images(covariance, w):
    freqs, block, wide = w.shape
    half = freqs // 2
    return pl.pallas_call(
        send_kernel,
        in_specs=[HBM, VMEM],
        out_specs=VMEM,
        scratch_shapes=block_scratch(half, block, wide),
        out_shape=jax.ShapeDtypeStruct((half, block, wide), jnp.float32),
        name="send_images",
        compiler_params=PARAMS,
    )(covariance, w)


def own_form(cov, w, w2_ref, stream):
    block, wide = w2_ref.shape
    slab = wide // 2
    tile = block // 2
    turned(w, w2_ref, tile)
    total = jnp.zeros((1, wide), jnp.float32)
    for t in range(2):
        stream.take()
        rows = slice(t * tile, (t + 1) * tile)
        left = w[rows].astype(jnp.float32)
        image = dot(cov[0, rows, rows], w[rows])
        cross = dot(cov[1, rows, rows], w[rows, :slab])
        if t == 0:
            rest = slice(tile, block)
            upper = dot(cov[0, rows, rest], w[rest])
            upper += dot(cov[1, rows, rest], w2_ref[rest])
            image += 2.0 * upper
        total += row_sum(left * image)
        twice = 2.0 * row_sum(left[:, slab:] * cross)
        total += jnp.concatenate([twice, jnp.zeros_like(twice)], axis=1)
    return total


def own_forms(half, first, side, cov_ref, w_ref, quad_ref, buffer, w2_ref, sems, more=None):
    stream = block_stream(range(half), first, side, cov_ref, buffer, sems, True)
    for i in range(half):
        form = own_form(buffer.at[i], w_ref.at[first + i], w2_ref, stream)
        if more is not None:
            form += more(i)
        quad_ref[pl.ds(first + i, 1), :] = form


def keep_kernel(cov_ref, w_ref, image_ref, quad_ref, buffer, w2_ref, sems):
    place = Place(w_ref.shape[0])
    half = quad_ref.shape[0] // 2
    quad_ref[...] = jnp.zeros_like(quad_ref)

    @pl.when(place.diag)
    def _():
        own_forms(half, place.first, place.core, cov_ref, w_ref, quad_ref, buffer, w2_ref, sems)

    @pl.when(jnp.logical_not(place.diag))
    def _():
        images_of([0], place.first, place.core, cov_ref, w_ref, image_ref, buffer, w2_ref, sems)


def keep_images(covariance, w):
    freqs, block, wide = w.shape
    half = freqs // 2
    return pl.pallas_call(
        keep_kernel,
        in_specs=[HBM, VMEM],
        out_specs=[VMEM, VMEM],
        scratch_shapes=block_scratch(half, block, wide),
        out_shape=[
            jax.ShapeDtypeStruct((1, block, wide), jnp.float32),
            jax.ShapeDtypeStruct((freqs, wide), jnp.float32),
        ],
        name="keep_images",
        compiler_params=PARAMS,
    )(covariance, w)


def early_kernel(pieces, spare, n_left, quad_in_ref, cov_ref, w_ref, keep_ref, received_ref, *refs):
    lefts = refs[:n_left]
    out_ref, rest_ref, buffer, w2_ref, sems, image_ref = refs[n_left:]
    freqs, half, block = w_ref.shape[0], received_ref.shape[0], w_ref.shape[1]
    wide = out_ref.shape[1]
    place = Place(freqs)
    out_ref[...] = quad_in_ref[...]

    @pl.when(place.diag)
    def _():
        first = place.other

        def more(i):
            def pair(at, count):
                return w_ref[first + i, pl.ds(at, count)].astype(jnp.float32) * received_ref[i, pl.ds(at, count)]

            return 2.0 * folded(block, wide, pair)

        own_forms(half, first, place.core, cov_ref, w_ref, out_ref, buffer, w2_ref, sems, more)

    @pl.when(jnp.logical_not(place.diag))
    def _():
        to = 0
        images_of([1], place.first, place.core, cov_ref, w_ref, image_ref, buffer, w2_ref, sems)
        for i in range(half):
            own = (keep_ref, image_ref)[i]
            value = jnp.zeros((1, wide), jnp.float32)
            for source, rows, item, row in pieces:
                if item == i:

                    def far(at, count, source=source, row=row, i=i, own=own):
                        side = pl.ds(row + at, count)
                        return lefts[source][pl.ds(at, count)].astype(jnp.float32) * (
                            own[0, side] + received_ref[i, side]
                        )

                    value += folded(rows, wide, far)
            for item, row, rows in spare:
                if item == i:
                    side = slice(row, row + rows)
                    rest_ref[to : to + rows] = own[0, side] + received_ref[i, side]
                    to += rows
            out_ref[pl.ds(place.first + i, 1), :] += 2.0 * value


def early_dots(quad, covariance, w, keep, received, lefts, pieces, spare):
    _, block, wide = w.shape
    half = received.shape[0]
    left_over = sum(rows for _, _, rows in spare)
    return pl.pallas_call(
        functools.partial(early_kernel, pieces, spare, len(lefts)),
        in_specs=[VMEM, HBM] + [VMEM] * (3 + len(lefts)),
        out_specs=[VMEM, VMEM],
        scratch_shapes=[*block_scratch(half, block, wide), pltpu.VMEM((1, block, wide), jnp.float32)],
        out_shape=[
            jax.ShapeDtypeStruct(quad.shape, jnp.float32),
            jax.ShapeDtypeStruct((left_over, wide), jnp.float32),
        ],
        name="early_dots",
        compiler_params=PARAMS,
    )(quad, covariance, w, *map(resident, (keep, received, *lefts)))


def late_kernel(pieces, planes, own, quad_in_ref, norm_ref, rest_ref, *refs):
    lefts, (out_ref, quad_ref) = refs[:-2], refs[-2:]
    freqs, slab = norm_ref.shape
    place = Place(freqs)
    quad_ref[...] = quad_in_ref[...]

    @pl.when(jnp.logical_not(place.diag))
    def _():
        for source, at, rows, item, row in pieces:


            def far(k, count, source=source, at=at, row=row):
                return lefts[source][pl.ds(at + k, count)].astype(jnp.float32) * rest_ref[pl.ds(row + k, count)]

            quad_ref[pl.ds(place.first + item, 1), :] += 2.0 * folded(rows, quad_ref.shape[1], far)

    both = jnp.concatenate([quad_ref[:, :slab] + quad_ref[:, slab:], norm_ref[...]], axis=0)
    for owner in range(slab // own):
        parcel = both[:, owner * own : (owner + 1) * own]
        for z in range(planes):
            at = (owner * planes + z) * 2 * freqs
            out_ref[at : at + 2 * freqs, :own] = parcel


def late_dots(quad, norm, rest, lefts, pieces, owners, planes):
    freqs, slab = norm.shape
    wide = quad.shape[1]
    own = slab // owners
    return pl.pallas_call(
        functools.partial(late_kernel, pieces, planes, own),
        in_specs=[VMEM] * (3 + len(lefts)),
        out_specs=VMEM,
        scratch_shapes=[pltpu.VMEM((freqs, wide), jnp.float32)],
        out_shape=jax.ShapeDtypeStruct((owners * planes * 2 * freqs, -(-own // 128) * 128), jnp.float32),
        name="late_dots",
        compiler_params=PARAMS,
    )(quad, norm, *map(resident, (rest, *lefts)))


def finish_kernel(planes, arrived_ref, power_ref, surface_ref):
    freqs, own = power_ref.shape
    mine = lax.axis_index("freq")
    sources = arrived_ref.shape[0] // (planes * 2 * freqs)
    surface = jnp.zeros_like(surface_ref)
    for z in range(planes):
        total = jnp.zeros((2 * freqs, own), jnp.float32)
        for source in range(sources):
            at = (source * planes + z) * 2 * freqs
            total += arrived_ref[at : at + 2 * freqs, :own]
        power = total[:freqs] / total[freqs:]
        surface += row_sum(power)

        @pl.when(mine == z)
        def _():
            power_ref[...] = power

    surface_ref[...] = surface / (freqs * planes)


def finish(arrived, freqs, planes, own):
    return pl.pallas_call(
        functools.partial(finish_kernel, planes),
        in_specs=[VMEM],
        out_specs=[VMEM, VMEM],
        out_shape=[
            jax.ShapeDtypeStruct((freqs, own), jnp.float32),
            jax.ShapeDtypeStruct((1, own), jnp.float32),
        ],
        name="finish",
        compiler_params=PARAMS,
    )(resident(arrived))


def local(mesh, covariance, replica_table, slab_index):
    rows, cols, planes = (mesh.shape[a] for a in ("row", "col", "freq"))
    freqs, _, row_block, block = covariance.shape
    slab = slab_index.shape[0]
    chips = cols // 2
    if row_block != 2 * block or chips != rows or freqs != 4:
        raise ValueError("unsupported mesh")
    axes = ("row", "col")

    def device(r, q, j):
        return r * cols + 2 * q + j

    def move(x, pairs):
        return lax.ppermute(x, axes, pairs)

    def total(xs):
        return functools.reduce(jnp.add, xs)

    everyone = [(r, q, j) for r in range(rows) for q in range(chips) for j in range(2)]
    core_swap = [(device(r, q, j), device(r, q, 1 - j)) for r, q, j in everyone]

    n = RELAYED
    chunk = [block * c // 16 for c in CHUNKS]
    starts = [sum(chunk[:k]) for k in range(n + 1)]
    tail = block - starts[n]
    shifts = range(1, rows)
    pairs = {}
    for d in shifts:
        out, back, relay = [], [], []
        for r in range(rows):
            for j in range(2):
                other = (r + d) % rows
                out.append((device(r, r, j), device(r, other, j)))
                back.append((device(r, other, j), device(r, r, j)))
                relay.append((device(r, r, j), device(other, r, j)))
        pairs[d] = out, out + back, relay

    slab_index = apart(slab_index)
    replica_table = apart(replica_table)
    hops = {}
    for d in shifts:
        chunks = pick(slab_index, replica_table, d, rows, 0, chunk[:1], False)
        hops[d] = [move(chunks[0], pairs[d][1])]
    for d in shifts:
        sizes = [*chunk[1:], tail]
        chunks = pick(slab_index, replica_table, d, rows, chunk[0], sizes, True)
        hops[d] += [move(chunks[k - 1], pairs[d][1 if k < n else 0]) for k in range(1, n + 1)]

    w, norm = gather(slab_index, replica_table)
    w = resident(w)
    sent = send_images(covariance, w)
    received = move(sent, core_swap)
    relayed = [total([move(hops[d][k], pairs[d][2]) for d in shifts]) for k in range(n)]
    direct = [total([hops[d][k] for d in shifts]) for k in range(n + 1)]
    keep, quad = keep_images(covariance, w)
    early = [(k, chunk[k], 0, starts[k]) for k in range(n)]
    early += [(n + k, chunk[k], 1, starts[k]) for k in range(n - 1)]
    spare = [(0, starts[n], tail), (1, starts[n - 1], chunk[-1] + tail)]
    late = [(0, 0, tail, 0, 0), (0, tail, tail, 1, tail + chunk[-1]), (1, 0, chunk[-1], 1, tail)]
    quad, rest = early_dots(
        quad, covariance, w, keep, received, direct[:n] + relayed[: n - 1], early, spare
    )
    owners = rows * cols
    parcels = late_dots(quad, norm, rest, [direct[n], relayed[-1]], late, owners, planes)
    arrived = lax.all_to_all(parcels, ("row", "col", "freq"), 0, 0, tiled=True)
    power, surface = finish(arrived, freqs, planes, slab // owners)
    return power, surface[0]


def solution(mesh):
    in_specs = (P("freq", None, "row", "col"), P("freq", None, "col", None), P())
    out_specs = (P("freq", ("row", "col")), P(("row", "col")))

    def body(covariance, replica_table, slab_index):
        return local(mesh, covariance, replica_table, slab_index)

    return jax.shard_map(body, mesh=mesh, in_specs=in_specs, out_specs=out_specs, check_vma=False)
```

```python
import functools

import jax
import jax.numpy as jnp
from jax import lax
from jax.experimental import pallas as pl
from jax.experimental.pallas import tpu as pltpu
from jax.sharding import PartitionSpec as P


CHUNKS = (8, 9, 8)
RELAYED = len(CHUNKS)


PARAMS = pltpu.CompilerParams(vmem_limit_bytes=30 << 20)


HBM = pl.BlockSpec(memory_space=pltpu.HBM)
VMEM = pl.BlockSpec(memory_space=pltpu.VMEM)


def apart(x):
    return pltpu.with_memory_space_constraint(x, pltpu.HBM)


def resident(x):
    return pltpu.with_memory_space_constraint(x, pltpu.VMEM)


class Place:
    def __init__(self, freqs):
        row, col = lax.axis_index("row"), lax.axis_index("col")
        chip, core = col // 2, col % 2
        half = freqs // 2
        self.diag = row == chip
        self.on = (row == chip).astype(jnp.int32)
        self.core = core
        self.first = jnp.where(row == chip, core, (row > chip).astype(jnp.int32)) * half
        self.other = half - self.first
        self.row, self.chip, self.half = row, chip, half

    def sends(self, d, rows):
        to = (self.row + d) % rows
        direct = (self.row > to).astype(jnp.int32) * self.half
        relay = (self.chip > self.row).astype(jnp.int32) * self.half + self.half // 2
        return jnp.where(self.diag, direct, relay)


def dot(x, y):
    return jnp.dot(x, y, preferred_element_type=jnp.float32)


def row_sum(x):
    return jnp.sum(x, axis=0, keepdims=True)


def folded(rows, wide, product):
    def step(k, total):
        part = product(pl.multiple_of(k * 16, 16), 16)
        return total + (part[:8] + part[8:])

    return row_sum(lax.fori_loop(0, rows // 16, step, jnp.zeros((8, wide), jnp.float32), unroll=4))


def onehot_of(index_ref, grid_points):
    slab = index_ref.shape[0]
    points = lax.broadcasted_iota(jnp.int32, (grid_points, slab), 0)
    hit = points == index_ref[...].reshape(1, slab)
    return jnp.where(hit, 1.0, 0.0).astype(jnp.bfloat16)


def pick_kernel(sizes, index_ref, main_ref, *refs):
    slab = index_ref.shape[0]
    extra_ref, out_refs = (refs[0], refs[1:]) if len(refs) > len(sizes) else (None, refs)
    onehot = onehot_of(index_ref, main_ref.shape[3])
    start = 0
    for size, out_ref in zip(sizes, out_refs, strict=True):
        for part in range(2):
            columns = slice(part * slab, (part + 1) * slab)
            piece = dot(main_ref[0, part, start : start + size], onehot)
            out_ref[:size, columns] = piece.astype(jnp.bfloat16)
            if out_ref.shape[0] > size:
                piece = dot(extra_ref[0, part], onehot)
                out_ref[size:, columns] = piece.astype(jnp.bfloat16)
        start += size


def pick(index, table, d, rows, start, sizes, double_last):
    freqs, _, _, grid_points = table.shape
    slab = index.shape[0]
    shapes = [(n, 2 * slab) for n in sizes]
    height = sum(sizes)
    extra = sizes[-1]
    quarter = freqs // 4

    def main_at(i):
        return (Place(freqs).sends(d, rows), 0, start, 0)

    def extra_at(i):
        place = Place(freqs)
        return (jnp.where(place.diag, place.sends(d, rows) + quarter, 0), 0, start + height - extra, 0)

    def rows_of(height, at):
        element = pl.Element
        return pl.BlockSpec((element(1), element(2), element(height), element(grid_points)), at)

    specs = [pl.BlockSpec((slab,), lambda i: (0,)), rows_of(height, main_at)]
    args = [index, table]
    if double_last:
        shapes[-1] = (2 * extra, 2 * slab)
        specs.append(rows_of(extra, extra_at))
        args.append(table)
    return pl.pallas_call(
        functools.partial(pick_kernel, sizes),
        grid=(1,),
        in_specs=specs,
        out_specs=[pl.BlockSpec(s, lambda i: (0, 0)) for s in shapes],
        out_shape=[jax.ShapeDtypeStruct(s, jnp.bfloat16) for s in shapes],
        compiler_params=PARAMS,
    )(*args)


def fetch(source, target, sem):
    copy = pltpu.make_async_copy(source, target, sem)
    copy.start()
    return copy


def gather_kernel(index_ref, table_ref, w_ref, norm_ref, onehot_ref, buffer, sems):
    slab = index_ref.shape[0]
    freqs = norm_ref.shape[0]
    place = Place(freqs)

    def work(steps, at, with_norm):
        copies = [fetch(table_ref.at[at(i)], buffer.at[i], sems.at[i]) for i in range(steps)]
        onehot_ref[...] = onehot_of(index_ref, table_ref.shape[3])
        for i in range(steps):
            copies[i].wait()
            total = jnp.zeros((1, slab), jnp.float32)
            for part in range(2):
                piece = dot(buffer[i, part], onehot_ref[...])
                w_ref[at(i), :, part * slab : (part + 1) * slab] = piece.astype(jnp.bfloat16)
                if with_norm:
                    total += row_sum(piece * piece)
            if with_norm:
                norm_ref[i : i + 1, :] = total

    @pl.when(place.diag)
    def _():
        work(freqs, lambda i: i, True)

    @pl.when(jnp.logical_not(place.diag))
    def _():
        norm_ref[...] = jnp.zeros_like(norm_ref)
        work(freqs // 2, lambda i: place.first + i, False)


def gather(index, table):
    freqs, _, block, grid_points = table.shape
    slab = index.shape[0]
    return pl.pallas_call(
        gather_kernel,
        in_specs=[VMEM, HBM],
        out_specs=[VMEM, VMEM],
        out_shape=[
            jax.ShapeDtypeStruct((freqs, block, 2 * slab), jnp.bfloat16),
            jax.ShapeDtypeStruct((freqs, slab), jnp.float32),
        ],
        scratch_shapes=[
            pltpu.VMEM((grid_points, slab), jnp.bfloat16),
            pltpu.VMEM((freqs, 2, block, grid_points), jnp.bfloat16),
            pltpu.SemaphoreType.DMA((freqs,)),
        ],
        name="gather",
        compiler_params=PARAMS,
    )(resident(index), table)


def turned(w, w2_ref, start=0):
    slab = w2_ref.shape[1] // 2
    w2_ref[start:, :slab] = -w[start:, slab:]
    w2_ref[start:, slab:] = w[start:, :slab]


def block_copies(items, first, side, cov_ref, buffer, sems, triangle):
    block = buffer.shape[2]
    tile = block // 2
    parts = [(0, tile, 0), (tile, tile, tile)] if triangle else [(0, block, 0)]
    copies = []
    for i in items:
        for t, (row, rows, column) in enumerate(parts):
            columns = pl.ds(column, block - column)
            source = cov_ref.at[first + i, :, pl.ds(pl.multiple_of(side * block + row, tile), rows), columns]
            target = buffer.at[i, :, pl.ds(row, rows), columns]
            copies.append((i, fetch(source, target, sems.at[2 * i + t])))
    return copies


def arrive(copies, item):
    for i, copy in copies:
        if i == item:
            copy.wait()


def images_of(items, first, side, cov_ref, w_ref, image_ref, buffer, w2_ref, sems):
    copies = block_copies(items, first, side, cov_ref, buffer, sems, False)
    tile = buffer.shape[2] // 2
    for place, i in enumerate(items):
        w = w_ref.at[first + i]
        turned(w, w2_ref)
        arrive(copies, i)
        for t in range(2):
            rows = slice(t * tile, (t + 1) * tile)
            image_ref[place, rows] = dot(buffer[i, 0, rows], w[...]) + dot(buffer[i, 1, rows], w2_ref[...])


def send_kernel(cov_ref, w_ref, image_ref, buffer, w2_ref, sems):
    place = Place(w_ref.shape[0])
    images_of(range(image_ref.shape[0]), place.first, 1 - place.core, cov_ref, w_ref, image_ref, buffer, w2_ref, sems)


def block_scratch(half, block, wide):
    return [
        pltpu.VMEM((half, 2, block, block), jnp.bfloat16),
        pltpu.VMEM((block, wide), jnp.bfloat16),
        pltpu.SemaphoreType.DMA((2 * half,)),
    ]


def send_images(covariance, w):
    freqs, block, wide = w.shape
    half = freqs // 2
    return pl.pallas_call(
        send_kernel,
        in_specs=[HBM, VMEM],
        out_specs=VMEM,
        scratch_shapes=block_scratch(half, block, wide),
        out_shape=jax.ShapeDtypeStruct((half, block, wide), jnp.float32),
        name="send_images",
        compiler_params=PARAMS,
    )(covariance, w)


def own_form(cov, w, w2_ref):
    block, wide = w2_ref.shape
    slab = wide // 2
    tile = block // 2
    turned(w, w2_ref, tile)
    total = jnp.zeros((1, wide), jnp.float32)
    for t in range(2):
        rows = slice(t * tile, (t + 1) * tile)
        left = w[rows].astype(jnp.float32)
        image = dot(cov[0, rows, rows], w[rows])
        cross = dot(cov[1, rows, rows], w[rows, :slab])
        if t == 0:
            rest = slice(tile, block)
            upper = dot(cov[0, rows, rest], w[rest])
            upper += dot(cov[1, rows, rest], w2_ref[rest])
            image += 2.0 * upper
        total += row_sum(left * image)
        twice = 2.0 * row_sum(left[:, slab:] * cross)
        total += jnp.concatenate([twice, jnp.zeros_like(twice)], axis=1)
    return total


def own_forms(half, first, side, cov_ref, w_ref, quad_ref, buffer, w2_ref, sems, more=None):
    copies = block_copies(range(half), first, side, cov_ref, buffer, sems, True)
    for i in range(half):
        arrive(copies, i)
        form = own_form(buffer.at[i], w_ref.at[first + i], w2_ref)
        if more is not None:
            form += more(i)
        quad_ref[pl.ds(first + i, 1), :] = form


def keep_kernel(cov_ref, w_ref, image_ref, quad_ref, buffer, w2_ref, sems):
    place = Place(w_ref.shape[0])
    half = quad_ref.shape[0] // 2
    quad_ref[...] = jnp.zeros_like(quad_ref)

    @pl.when(place.diag)
    def _():
        own_forms(half, place.first, place.core, cov_ref, w_ref, quad_ref, buffer, w2_ref, sems)

    @pl.when(jnp.logical_not(place.diag))
    def _():
        images_of([0], place.first, place.core, cov_ref, w_ref, image_ref, buffer, w2_ref, sems)


def keep_images(covariance, w):
    freqs, block, wide = w.shape
    half = freqs // 2
    return pl.pallas_call(
        keep_kernel,
        in_specs=[HBM, VMEM],
        out_specs=[VMEM, VMEM],
        scratch_shapes=block_scratch(half, block, wide),
        out_shape=[
            jax.ShapeDtypeStruct((1, block, wide), jnp.float32),
            jax.ShapeDtypeStruct((freqs, wide), jnp.float32),
        ],
        name="keep_images",
        compiler_params=PARAMS,
    )(covariance, w)


def early_kernel(pieces, spare, n_left, quad_in_ref, cov_ref, w_ref, keep_ref, received_ref, *refs):
    lefts = refs[:n_left]
    out_ref, rest_ref, buffer, w2_ref, sems, image_ref = refs[n_left:]
    freqs, half, block = w_ref.shape[0], received_ref.shape[0], w_ref.shape[1]
    wide = out_ref.shape[1]
    place = Place(freqs)
    out_ref[...] = quad_in_ref[...]

    @pl.when(place.diag)
    def _():
        first = place.other

        def more(i):
            def pair(at, count):
                return w_ref[first + i, pl.ds(at, count)].astype(jnp.float32) * received_ref[i, pl.ds(at, count)]

            return 2.0 * folded(block, wide, pair)

        own_forms(half, first, place.core, cov_ref, w_ref, out_ref, buffer, w2_ref, sems, more)

    @pl.when(jnp.logical_not(place.diag))
    def _():
        to = 0
        images_of([1], place.first, place.core, cov_ref, w_ref, image_ref, buffer, w2_ref, sems)
        for i in range(half):
            own = (keep_ref, image_ref)[i]
            value = jnp.zeros((1, wide), jnp.float32)
            for source, rows, item, row in pieces:
                if item == i:

                    def far(at, count, source=source, row=row, i=i, own=own):
                        side = pl.ds(row + at, count)
                        return lefts[source][pl.ds(at, count)].astype(jnp.float32) * (
                            own[0, side] + received_ref[i, side]
                        )

                    value += folded(rows, wide, far)
            for item, row, rows in spare:
                if item == i:
                    side = slice(row, row + rows)
                    rest_ref[to : to + rows] = own[0, side] + received_ref[i, side]
                    to += rows
            out_ref[pl.ds(place.first + i, 1), :] += 2.0 * value


def early_dots(quad, covariance, w, keep, received, lefts, pieces, spare):
    _, block, wide = w.shape
    half = received.shape[0]
    left_over = sum(rows for _, _, rows in spare)
    return pl.pallas_call(
        functools.partial(early_kernel, pieces, spare, len(lefts)),
        in_specs=[VMEM, HBM] + [VMEM] * (3 + len(lefts)),
        out_specs=[VMEM, VMEM],
        scratch_shapes=[*block_scratch(half, block, wide), pltpu.VMEM((1, block, wide), jnp.float32)],
        out_shape=[
            jax.ShapeDtypeStruct(quad.shape, jnp.float32),
            jax.ShapeDtypeStruct((left_over, wide), jnp.float32),
        ],
        name="early_dots",
        compiler_params=PARAMS,
    )(quad, covariance, w, *map(resident, (keep, received, *lefts)))


def late_kernel(pieces, planes, own, quad_in_ref, norm_ref, rest_ref, *refs):
    lefts, (out_ref, quad_ref) = refs[:-2], refs[-2:]
    freqs, slab = norm_ref.shape
    place = Place(freqs)
    quad_ref[...] = quad_in_ref[...]

    @pl.when(jnp.logical_not(place.diag))
    def _():
        for source, at, rows, item, row in pieces:


            def far(k, count, source=source, at=at, row=row):
                return lefts[source][pl.ds(at + k, count)].astype(jnp.float32) * rest_ref[pl.ds(row + k, count)]

            quad_ref[pl.ds(place.first + item, 1), :] += 2.0 * folded(rows, quad_ref.shape[1], far)

    quad, norm = quad_ref[:, :slab] + quad_ref[:, slab:], norm_ref[...]
    for owner in range(slab // own):
        mine = slice(owner * own, (owner + 1) * own)
        parcel = jnp.concatenate([quad[:, mine], norm[:, mine]], axis=1)
        for z in range(planes):
            out_ref[owner * planes + z, :, : 2 * own] = parcel


def late_dots(quad, norm, rest, lefts, pieces, owners, planes):
    freqs, slab = norm.shape
    wide = quad.shape[1]
    own = slab // owners
    return pl.pallas_call(
        functools.partial(late_kernel, pieces, planes, own),
        in_specs=[VMEM] * (3 + len(lefts)),
        out_specs=VMEM,
        scratch_shapes=[pltpu.VMEM((freqs, wide), jnp.float32)],
        out_shape=jax.ShapeDtypeStruct((owners * planes, freqs, -(-2 * own // 128) * 128), jnp.float32),
        name="late_dots",
        compiler_params=PARAMS,
    )(quad, norm, *map(resident, (rest, *lefts)))


def finish_kernel(planes, arrived_ref, power_ref, surface_ref):
    freqs, own = power_ref.shape
    mine = lax.axis_index("freq")
    surface = jnp.zeros_like(surface_ref)
    for z in range(planes):
        total = arrived_ref[z]
        for source in range(planes + z, arrived_ref.shape[0], planes):
            total += arrived_ref[source]
        power = total[:, :own] / total[:, own : 2 * own]
        surface += row_sum(power)

        @pl.when(mine == z)
        def _():
            power_ref[...] = power

    surface_ref[...] = surface / (freqs * planes)


def finish(arrived, freqs, planes, own):
    return pl.pallas_call(
        functools.partial(finish_kernel, planes),
        in_specs=[VMEM],
        out_specs=[VMEM, VMEM],
        out_shape=[
            jax.ShapeDtypeStruct((freqs, own), jnp.float32),
            jax.ShapeDtypeStruct((1, own), jnp.float32),
        ],
        name="finish",
        compiler_params=PARAMS,
    )(resident(arrived))


def local(mesh, covariance, replica_table, slab_index):
    rows, cols, planes = (mesh.shape[a] for a in ("row", "col", "freq"))
    freqs, _, row_block, block = covariance.shape
    slab = slab_index.shape[0]
    chips = cols // 2
    if row_block != 2 * block or chips != rows or freqs != 4:
        raise ValueError("unsupported mesh")
    axes = ("row", "col")

    def device(r, q, j):
        return r * cols + 2 * q + j

    def move(x, pairs):
        return lax.ppermute(x, axes, pairs)

    def total(xs):
        return functools.reduce(jnp.add, xs)

    everyone = [(r, q, j) for r in range(rows) for q in range(chips) for j in range(2)]
    core_swap = [(device(r, q, j), device(r, q, 1 - j)) for r, q, j in everyone]

    n = RELAYED
    chunk = [block * c // 32 // 16 * 16 for c in CHUNKS]
    starts = [sum(chunk[:k]) for k in range(n + 1)]
    tail = block - starts[n]
    shifts = range(1, rows)
    pairs = {}
    for d in shifts:
        out, back, relay = [], [], []
        for r in range(rows):
            for j in range(2):
                other = (r + d) % rows
                out.append((device(r, r, j), device(r, other, j)))
                back.append((device(r, other, j), device(r, r, j)))
                relay.append((device(r, r, j), device(other, r, j)))
        pairs[d] = out, out + back, relay

    slab_index = apart(slab_index)
    replica_table = apart(replica_table)
    hops = {}
    for d in shifts:
        chunks = pick(slab_index, replica_table, d, rows, 0, chunk[:1], False)
        hops[d] = [move(chunks[0], pairs[d][1])]
    for d in shifts:
        sizes = [*chunk[1:], tail]
        chunks = pick(slab_index, replica_table, d, rows, chunk[0], sizes, True)
        hops[d] += [move(chunks[k - 1], pairs[d][1 if k < n else 0]) for k in range(1, n + 1)]

    w, norm = gather(slab_index, replica_table)
    w = resident(w)
    sent = send_images(covariance, w)
    received = move(sent, core_swap)
    relayed = [total([move(hops[d][k], pairs[d][2]) for d in shifts]) for k in range(n)]
    direct = [total([hops[d][k] for d in shifts]) for k in range(n + 1)]
    keep, quad = keep_images(covariance, w)
    hold = n - 2
    early = [(k, chunk[k], 0, starts[k]) for k in range(n)]
    early += [(n + k, chunk[k], 1, starts[k]) for k in range(hold)]
    spare = [(0, starts[n], tail), (1, starts[hold], block - starts[hold])]
    late = [(0, 0, tail, 0, 0), (0, tail, tail, 1, tail + starts[n] - starts[hold])]
    late += [(1 + k - hold, 0, chunk[k], 1, tail + starts[k] - starts[hold]) for k in range(hold, n)]
    quad, rest = early_dots(
        quad, covariance, w, keep, received, direct[:n] + relayed[:hold], early, spare
    )
    owners = rows * cols
    parcels = late_dots(quad, norm, rest, [direct[n], *relayed[hold:]], late, owners, planes)
    arrived = lax.all_to_all(parcels, ("row", "col", "freq"), 0, 0, tiled=True)
    power, surface = finish(arrived, freqs, planes, slab // owners)
    return power, surface[0]


def solution(mesh):
    in_specs = (P("freq", None, "row", "col"), P("freq", None, "col", None), P())
    out_specs = (P("freq", ("row", "col")), P(("row", "col")))

    def body(covariance, replica_table, slab_index):
        return local(mesh, covariance, replica_table, slab_index)

    return jax.shard_map(body, mesh=mesh, in_specs=in_specs, out_specs=out_specs, check_vma=False)
```
